32 devices in a mesh: pts: 8 (over z, y), feat: 4 (over x, core).
Axes of the slice: x: 2, y: 2, z: 4, core: 2. Of those that a mesh axis runs over, the one named last changes fastest.
Arguments:
- slab: bfloat16 [16384, 768], P('pts', 'feat'), may hold values from -40 to 40
- centres: bfloat16 [4096, 768], replicated, may hold values from -3 to 3
- labels: int32 [16384, 1], P(('pts', 'feat')), may hold values from 0 to 4095
- sample_rows: int32 [8, 8, 4], P('pts'), may hold values from 0 to 2047, as said below
- sample_count: int32 [8, 8], P('pts'), may hold values from 0 to 4, as said below
- slot_offset: int32 [8, 8], P('pts'), may hold values from 0 to 28, as said below
Outputs:
- coreset: bfloat16 [256, 768], P('pts', 'feat')
The draws below stay inside these ranges and needn't reach their ends.
Inputs may be any that keep to these rules, and one draw needn't show every extreme that they name: `sample_rows`: row indices within a source shard; sampled independently with replacement. `sample_count`: in every draw some owner receives 4 rows from every source. slot_offset[o,p] is the sum of sample_count[q,o] over sources q < p.
All inputs are finite; a program needn't handle non-finite values.
Results may differ from the reference program's by a relative error of at most 0.0006.
Values may be sent and summed in bfloat16 or wider, within the bound.
A program may use at most 64 MiB of HBM per device.

```python
import math
import jax
import jax.numpy as jnp
from jax import lax

D = 768
CENTRES = 4096
CAP = 4
ROWS_PTS = 2048
NPTS = 16384
SOURCES = 8
OWNERS = 8
OWN_CAP = 32


def draw_slab(key, part):
    key_base, key_row, key_col = jax.random.split(key, 3)
    row_scale = jnp.exp(jax.random.uniform(key_row, (NPTS, 1), jnp.float32, math.log(0.3), math.log(3.0)))
    col_scale = jnp.exp(jax.random.uniform(key_col, (1, D), jnp.float32, math.log(0.3), math.log(3.0))) / 1.4
    base_vals = jax.random.normal(key_base, (NPTS, D), jnp.float32)
    return jnp.clip(base_vals * row_scale * col_scale, -40.0, 40.0).astype(jnp.bfloat16)


def plan_full(key):
    return jax.random.randint(jax.random.fold_in(key, 7), (), 0, OWNERS, jnp.int32)


def plan_counts(key):
    base_key = jax.random.fold_in(key, 11)
    key_heavy, key_light, key_busy = jax.random.split(base_key, 3)
    heavy = jax.random.randint(key_heavy, (OWNERS,), 0, 4, jnp.int32) == 0
    light_counts = jax.random.randint(key_light, (SOURCES, OWNERS), 0, CAP, jnp.int32)
    busy_counts = jax.random.randint(key_busy, (SOURCES, OWNERS), 2, CAP + 1, jnp.int32)
    counts_all = jnp.where(heavy[None, :], busy_counts, light_counts)
    full_owner = plan_full(key)
    owner_ids = jnp.arange(OWNERS, dtype=jnp.int32)[None, :]
    return jnp.where(owner_ids == full_owner, jnp.int32(CAP), counts_all).astype(jnp.int32)


def draw_sample_count(key, part):
    return plan_counts(key)


def draw_slot_offset(key, part):
    per_owner = plan_counts(key).T
    return (jnp.cumsum(per_owner, axis=1) - per_owner).astype(jnp.int32)


def draw_sample_rows(key, part):
    row_key = jax.random.fold_in(key, 23)
    picked = jax.random.randint(row_key, (SOURCES, OWNERS, CAP), 0, ROWS_PTS, jnp.int32)
    full_owner = plan_full(key)
    owner_ids = jnp.arange(OWNERS, dtype=jnp.int32)[None, :, None]
    slot_ids = jnp.arange(CAP, dtype=jnp.int32)[None, None, :]
    source_ids = jnp.arange(SOURCES, dtype=jnp.int32)[:, None, None]
    top_spot = (owner_ids == full_owner) & (slot_ids == 0) & (source_ids == 0)
    low_spot = (owner_ids == full_owner) & (slot_ids == 1) & (source_ids == 0)
    picked = jnp.where(top_spot, jnp.int32(ROWS_PTS - 1), picked)
    return jnp.where(low_spot, jnp.int32(0), picked).astype(jnp.int32)


def touch_ends(drawn, key, least, largest):
    place = [jax.random.randint(jax.random.fold_in(key, axis), (), 0, length) for axis, length in enumerate(drawn.shape)]
    main_axis = drawn.shape.index(max(drawn.shape))
    next_to = place[:main_axis] + [(place[main_axis] + 1) % drawn.shape[main_axis]] + place[main_axis + 1:]
    return drawn.at[tuple(place)].set(least).at[tuple(next_to)].set(largest)


def gaussian(rng, dims, deviation, limit, held_as=jnp.bfloat16):
    drawn = deviation * jax.random.normal(rng, dims, jnp.float32)
    return jnp.clip(drawn, min=-limit, max=limit).astype(held_as)


def setup_inputs(seed: int = 0) -> dict:
    keys = jax.random.split(jax.random.key(seed), 7)
    slab = draw_slab(jax.random.fold_in(keys[6], 71), 0)
    centres = gaussian(keys[1], (CENTRES, D), 0.5, 3.0)
    labels = touch_ends(jax.random.randint(keys[2], (NPTS, 1), 0, CENTRES), jax.random.fold_in(keys[2], 1), 0, CENTRES - 1).astype(jnp.int32)
    sample_rows = draw_sample_rows(jax.random.fold_in(keys[6], 71), 0)
    sample_count = draw_sample_count(jax.random.fold_in(keys[6], 71), 0)
    slot_offset = draw_slot_offset(jax.random.fold_in(keys[6], 71), 0)
    return {"slab": slab, "centres": centres, "labels": labels, "sample_rows": sample_rows, "sample_count": sample_count, "slot_offset": slot_offset}


def nearest_block(points, centres, centre_sq):
    cross_term = jnp.dot(points, centres.T, preferred_element_type=jnp.float32)
    point_sq = jnp.sum(jnp.square(points.astype(jnp.float32)), axis=1)
    return jnp.min(point_sq[:, None] + centre_sq[None, :] - 2.0 * cross_term, axis=1)


def reference(slab, centres, labels, sample_rows, sample_count, slot_offset):
    centre_sq = jnp.sum(jnp.square(centres.astype(jnp.float32)), axis=1)
    blocks = slab.reshape(NPTS // ROWS_PTS, ROWS_PTS, D)
    nearest = lax.map(lambda span_rows: nearest_block(span_rows, centres, centre_sq), blocks).reshape(NPTS)
    member = labels[:, 0]
    cluster_cost = jax.ops.segment_sum(nearest, member, num_segments=CENTRES)
    cluster_size = jax.ops.segment_sum(jnp.ones_like(nearest), member, num_segments=CENTRES)
    sens = nearest / cluster_cost[member] + 1.0 / cluster_size[member]
    weight = (2.0 * CENTRES / NPTS) / sens
    global_rows = jnp.arange(SOURCES, dtype=jnp.int32)[:, None, None] * ROWS_PTS + sample_rows.astype(jnp.int32)
    chosen = slab[global_rows]
    chosen_weight = weight[global_rows]
    live_slot = jnp.arange(CAP, dtype=jnp.int32)[None, None, :] < sample_count[:, :, None]
    scaled = jnp.where(live_slot[..., None], chosen.astype(jnp.float32) * chosen_weight[..., None], jnp.float32(0.0)).astype(jnp.bfloat16)
    target = (jnp.arange(OWNERS, dtype=jnp.int32)[None, :, None] * OWN_CAP
              + slot_offset.T.astype(jnp.int32)[:, :, None]
              + jnp.arange(CAP, dtype=jnp.int32)[None, None, :])
    placed = jnp.zeros((OWNERS * OWN_CAP, D), jnp.float32)
    placed = placed.at[target.reshape(-1)].add(scaled.reshape(-1, D).astype(jnp.float32), mode="drop")
    return placed.astype(jnp.bfloat16)
```

```python
import functools

import jax
import jax.numpy as jnp
from jax import lax
from jax.experimental import pallas as pl
from jax.experimental.pallas import tpu as pltpu
from jax.sharding import PartitionSpec as P

NT = (((1,), (1,)), ((), ()))
LANES = 128
HALF = LANES // 2
SUB = 8
MESH = pl.DeviceIdType.MESH


def local(slab, centres, labels, sample_rows, sample_count, slot_offset):
    rows_pts, feat_width = slab.shape
    feat_count = lax.axis_size("feat")
    rows_dev = rows_pts // feat_count
    centre_count = centres.shape[0]
    centre_sq = jnp.sum(jnp.square(centres.astype(jnp.float32)), axis=1)
    stacked = slab.reshape(feat_count, rows_dev, feat_width)
    points = lax.all_to_all(stacked, "feat", split_axis=0, concat_axis=2, tiled=True)[0]
    cross_term = lax.dot_general(points, centres, NT, preferred_element_type=jnp.float32)
    point_sq = jnp.sum(jnp.square(points.astype(jnp.float32)), axis=1)
    nearest = jnp.min(point_sq[:, None] + centre_sq[None, :] - 2.0 * cross_term, axis=1)[None, :][0]
    member = labels[:, 0]
    cost_part = jax.ops.segment_sum(nearest, member, num_segments=centre_count)
    size_part = jax.ops.segment_sum(jnp.ones_like(nearest), member, num_segments=centre_count)
    cluster_cost, cluster_size = lax.psum((cost_part, size_part), ("pts", "feat"))
    own_sens = nearest / jnp.take(cluster_cost, member) + 1.0 / jnp.take(cluster_size, member)
    shard_sens = lax.all_gather(own_sens, "feat", axis=0, tiled=True)
    total_points = rows_pts * lax.axis_size("pts")
    weight = 2.0 * centre_count / total_points / shard_sens
    picked_rows = sample_rows[0]
    owner_count, slot_count = picked_rows.shape
    chosen = jnp.take(slab, picked_rows.reshape(-1), axis=0).reshape(
        owner_count, slot_count, feat_width
    )
    chosen_weight = jnp.take(weight, picked_rows)
    live_slot = jnp.arange(slot_count, dtype=jnp.int32)[None, :] < sample_count[0][:, None]
    scaled = jnp.where(
        live_slot[:, :, None], chosen.astype(jnp.float32) * chosen_weight[:, :, None], 0.0
    ).astype(jnp.bfloat16)
    arrived = lax.all_to_all(scaled, "pts", split_axis=0, concat_axis=0, tiled=True)
    target = slot_offset[0][:, None] + jnp.arange(slot_count, dtype=jnp.int32)[None, :]
    own_rows = arrived.shape[0] * slot_count
    placed = jnp.zeros((own_rows, feat_width), jnp.float32)
    placed = placed.at[target.reshape(-1)].add(
        arrived.reshape(-1, feat_width).astype(jnp.float32), mode="drop"
    )
    return placed.astype(jnp.bfloat16)


def kernel(n_p, n_f, chunks, tile, slab_ref, labels_ref, rows_ref, count_ref, offset_ref, cen_hbm,
           out_ref, cen, csq, pack_a, pack_b, got_a, got_b, lab_msg, lab_all, row_msg, row_all,
           red_msg, red_all, cen_sem, a_send, a_recv, b_send, b_recv, lab_send, lab_recv,
           row_send, row_recv, red_send, red_recv):
    f32, bf16 = jnp.float32, jnp.bfloat16
    rows_pts, width = slab_ref.shape
    rows_dev = rows_pts // n_f
    crow = rows_dev // chunks
    hrow = crow // 2
    n = n_p * n_f
    centre_count = cen.shape[0]
    slots = rows_ref.shape[2]
    tiles = centre_count // tile
    my_p, my_f = lax.axis_index("pts"), lax.axis_index("feat")
    me = my_p * n_f + my_f

    def device(d):
        other = lax.rem(me + d, n)
        return other // n_f, lax.rem(other, n_f)

    barrier = pltpu.get_barrier_semaphore()
    for d in range(1, n):
        pl.semaphore_signal(barrier, inc=1, device_id=device(d), device_id_type=MESH)

    cen_copies = []
    for t in range(tiles):
        part = pl.ds(t * tile, tile)
        copy = pltpu.make_async_copy(cen_hbm.at[part], cen.at[part], cen_sem.at[t])
        copy.start()
        cen_copies.append(copy)

    odd = lax.rem(my_f, 2)

    @pl.loop(0, n_f * chunks)
    def _(j):
        base = pl.multiple_of(j * crow, crow)
        left = slab_ref[pl.ds(base, crow), :LANES].astype(f32)
        right = slab_ref[pl.ds(base, crow), LANES:width].astype(f32)
        right = jnp.concatenate([right, right], axis=1)
        turned = pltpu.roll(left, HALF, 1)
        low = lax.broadcasted_iota(jnp.int32, (crow, LANES), 1) < HALF
        is_odd = jnp.full((crow, LANES), odd, jnp.int32) == 1
        main = jnp.where(is_odd, jnp.where(low, turned, right), left)
        rest = jnp.where(is_odd, jnp.where(low, left, turned), right)
        pack_a[pl.ds(base, crow), :] = main.astype(bf16)
        both = jnp.where(low[:hrow], rest[:hrow], rest[hrow:])
        pack_b[pl.ds(pl.multiple_of(j * hrow, hrow), hrow), :] = both.astype(bf16)

    pl.semaphore_wait(barrier, n - 1)

    slab_copies = []
    order = [e for e in range(2, n_f)] + [1]
    for c in range(chunks):
        copies = []
        for e in order:
            peer = lax.rem(my_f + e, n_f)
            at = pl.multiple_of(peer * rows_dev + c * crow, crow)
            half_at = pl.multiple_of(peer * (rows_dev // 2) + c * hrow, hrow)
            copies.append(pltpu.make_async_remote_copy(
                src_ref=pack_a.at[pl.ds(at, crow)], dst_ref=got_a.at[my_f, pl.ds(c * crow, crow)],
                send_sem=a_send.at[c, e - 1], recv_sem=a_recv.at[c, e - 1],
                device_id=(my_p, peer), device_id_type=MESH))
            copies.append(pltpu.make_async_remote_copy(
                src_ref=pack_b.at[pl.ds(half_at, hrow)], dst_ref=got_b.at[my_f, pl.ds(c * hrow, hrow)],
                send_sem=b_send.at[c, e - 1], recv_sem=b_recv.at[c, e - 1],
                device_id=(my_p, peer), device_id_type=MESH))
        for copy in copies:
            copy.start()
        slab_copies.append(copies)
    got_a[my_f] = pack_a[pl.ds(pl.multiple_of(my_f * rows_dev, rows_dev), rows_dev), :]
    got_b[my_f] = pack_b[pl.ds(pl.multiple_of(my_f * (rows_dev // 2), rows_dev // 2), rows_dev // 2), :]

    queries = n_p * SUB
    query_sub = lax.broadcasted_iota(jnp.int32, (queries, 1), 0)
    picked = jnp.full((queries, 1), -1, jnp.int32)
    for o in range(n_p):
        for s in range(slots):
            picked = jnp.where(query_sub == o * SUB + s, rows_ref[0, o, s], picked)
    members = labels_ref[...].astype(f32)
    lane_dev = lax.broadcasted_iota(jnp.int32, (queries, rows_dev), 1)
    own_hit = (lane_dev + my_f * rows_dev) == picked
    own_label = jnp.sum(jnp.where(own_hit, members + 1.0, 0.0), axis=1, keepdims=True)
    query_diag = (lax.broadcasted_iota(jnp.int32, (queries, LANES), 0)
                  == lax.broadcasted_iota(jnp.int32, (queries, LANES), 1))
    label_row = jnp.sum(jnp.where(query_diag, own_label, 0.0), axis=0, keepdims=True)
    lab_msg[...] = label_row
    lab_all[me] = label_row

    lab_copies = []
    for d in range(1, n):
        copy = pltpu.make_async_remote_copy(
            src_ref=lab_msg, dst_ref=lab_all.at[me], send_sem=lab_send.at[d - 1],
            recv_sem=lab_recv.at[d - 1], device_id=device(d), device_id_type=MESH)
        copy.start()
        lab_copies.append(copy)

    lane_pts = lax.broadcasted_iota(jnp.int32, (queries, rows_pts), 1)
    chosen = jnp.where(lane_pts == picked, 1.0, 0.0).astype(bf16)
    chosen = jnp.dot(chosen, slab_ref[...], preferred_element_type=f32)
    live = jnp.zeros((queries, 1), f32)
    for o in range(n_p):
        for s in range(slots):
            flag = jnp.where(count_ref[0, o] > s, 1.0, 0.0)
            live = jnp.where(query_sub == o * SUB + slots + s, flag, live)
    is_row = lax.rem(lax.broadcasted_iota(jnp.int32, (queries, width), 0), SUB) < slots
    sent = jnp.where(is_row, chosen, live)
    row_msg[:, :, :width] = sent.reshape(n_p, SUB, width)
    row_all[my_p] = row_msg[my_p]
    row_copies = []
    for d in range(1, n_p):
        owner = lax.rem(my_p + d, n_p)
        copy = pltpu.make_async_remote_copy(
            src_ref=row_msg.at[owner], dst_ref=row_all.at[my_p], send_sem=row_send.at[d - 1],
            recv_sem=row_recv.at[d - 1], device_id=(owner, my_f), device_id_type=MESH)
        copy.start()
        row_copies.append(copy)

    for t in range(tiles):
        cen_copies[t].wait()

    @pl.loop(0, tiles)
    def _(t):
        part = pl.ds(pl.multiple_of(t * tile, tile), tile)
        total = jnp.zeros((tile, LANES), f32)
        for b in range(cen.shape[1] // LANES):
            piece = cen[part, b * LANES:(b + 1) * LANES].astype(f32)
            total += piece * piece
        csq[part, :] = jnp.broadcast_to(jnp.sum(total, axis=1, keepdims=True), (tile, LANES))

    for copy in lab_copies:
        copy.wait()
    lanes = lax.broadcasted_iota(jnp.int32, (queries, LANES), 1)
    slot = lax.rem(lax.broadcasted_iota(jnp.int32, (queries, LANES), 0), SUB)
    is_slot = slot < slots
    wanted = []
    sums = jnp.zeros((queries, LANES), f32)
    span = n_p * slots
    for p in range(n_p):
        row = lab_all[p * n_f]
        for g in range(1, n_f):
            row = row + lab_all[p * n_f + g]
        want = jnp.sum(jnp.where(query_diag, row, 0.0), axis=1, keepdims=True) - 1.0
        wanted.append(want)
        size = jnp.sum(jnp.where(want == members, 1.0, 0.0), axis=1, keepdims=True)
        sums = jnp.where(is_slot & (lanes == span + p * slots + slot), size, sums)

    ones = jnp.ones((SUB, cen.shape[1]), bf16)
    near_parts = []
    for c in range(chunks):
        for copy in slab_copies[c]:
            copy.wait_recv()
        rows = pl.ds(c * crow, crow)
        half_rows = pl.ds(c * hrow, hrow)
        low = lax.broadcasted_iota(jnp.int32, (hrow, LANES), 1) < HALF
        blocks = []
        for pair in range(n_f // 2):
            even_b = got_b[2 * pair, half_rows].astype(f32)
            odd_b = got_b[2 * pair + 1, half_rows].astype(f32)
            top = jnp.where(low, even_b, pltpu.roll(odd_b, HALF, 1))
            bottom = jnp.where(low, pltpu.roll(even_b, HALF, 1), odd_b)
            middle = jnp.concatenate([top, bottom], axis=0).astype(bf16)
            blocks += [got_a[2 * pair, rows], middle, got_a[2 * pair + 1, rows]]
        points = jnp.concatenate(blocks, axis=1)
        wide = points.astype(f32)
        wide = wide * wide
        high = wide.astype(bf16)
        rest = (wide - high.astype(f32)).astype(bf16)
        point_sq = (lax.dot_general(ones, high, NT, preferred_element_type=f32)
                    + lax.dot_general(ones, rest, NT, preferred_element_type=f32))[:1]

        def step(t, best):
            part = pl.ds(pl.multiple_of(t * tile, tile), tile)
            cross = lax.dot_general(cen[part, :], points, NT, preferred_element_type=f32)
            square = csq[part, :]
            gap = jnp.concatenate([square] * (crow // LANES), axis=1) - 2.0 * cross
            return jnp.minimum(best, jnp.min(gap.reshape(tile // SUB, SUB, crow), axis=0))

        best = lax.fori_loop(0, tiles, step, jnp.full((SUB, crow), jnp.inf, f32))
        near_parts.append(point_sq + jnp.min(best, axis=0, keepdims=True))
    nearest = jnp.concatenate(near_parts, axis=1)

    for p in range(n_p):
        cost = jnp.sum(jnp.where(wanted[p] == members, nearest, 0.0), axis=1, keepdims=True)
        sums = jnp.where(is_slot & (lanes == p * slots + slot), cost, sums)
    own_near = jnp.sum(jnp.where(own_hit, nearest, 0.0), axis=1, keepdims=True)
    sums = jnp.where(is_slot & (lanes == 2 * span + my_p * slots + slot), own_near, sums)
    to_owner = jnp.sum(jnp.where(is_slot, sums, 0.0).reshape(n_p, SUB, LANES), axis=1, keepdims=True)
    red_msg[...] = to_owner
    red_all[0] = red_msg[my_p]
    red_copies = []
    for d in range(1, n):
        to = device(d)
        copy = pltpu.make_async_remote_copy(
            src_ref=red_msg.at[to[0]], dst_ref=red_all.at[d], send_sem=red_send.at[d - 1],
            recv_sem=red_recv.at[d - 1], device_id=to, device_id_type=MESH)
        copy.start()
        red_copies.append(copy)
    for copy in row_copies:
        copy.wait()
    for copies in slab_copies:
        for copy in copies:
            copy.wait_send()
    for copy in red_copies:
        copy.wait()
    total = jnp.broadcast_to(jnp.sum(red_all[...], axis=0), (SUB, LANES))
    size = pltpu.roll(total, LANES - span, 1)
    near = pltpu.roll(total, LANES - 2 * span, 1)
    weight = (2.0 * centre_count / (rows_pts * n_p)) / (near / total + 1.0 / size)
    sub = lax.broadcasted_iota(jnp.int32, (SUB, LANES), 0)
    lane = lax.broadcasted_iota(jnp.int32, (SUB, LANES), 1)
    out_rows = out_ref.shape[0]
    out_iota = lax.broadcasted_iota(jnp.int32, (out_rows, width), 0)
    placed = jnp.zeros((out_rows, width), f32)
    for p in range(n_p):
        mine = (sub < slots) & (lane == p * slots + sub)
        factor = jnp.sum(jnp.where(mine, weight, 0.0), axis=1, keepdims=True)
        block = row_all[p][:, :width]
        scaled = (block * factor).astype(bf16).astype(f32)
        for s in range(slots):
            flag = block[slots + s:slots + s + 1] > 0.5
            hit = (out_iota == offset_ref[0, p] + s) & flag
            placed = jnp.where(hit, scaled[s:s + 1], placed)
    out_ref[...] = placed.astype(bf16)


def fused(n_p, n_f, slab, centres, labels, sample_rows, sample_count, slot_offset):
    rows_pts, width = slab.shape
    rows_dev = rows_pts // n_f
    centre_count, depth = centres.shape
    slots = sample_rows.shape[2]
    chunks = 2
    tile = 512
    tiles = centre_count // tile
    n = n_p * n_f
    wide = pl.cdiv(width, LANES) * LANES
    vmem, smem = pl.BlockSpec(memory_space=pltpu.VMEM), pl.BlockSpec(memory_space=pltpu.SMEM)
    dma = pltpu.SemaphoreType.DMA
    return pl.pallas_call(
        functools.partial(kernel, n_p, n_f, chunks, tile),
        out_shape=jax.ShapeDtypeStruct((n_p * slots, width), jnp.bfloat16),
        in_specs=[vmem, vmem, smem, smem, smem, pl.BlockSpec(memory_space=pl.ANY)],
        out_specs=vmem,
        scratch_shapes=[
            pltpu.VMEM((centre_count, depth), jnp.bfloat16),
            pltpu.VMEM((centre_count, LANES), jnp.float32),
            pltpu.VMEM((rows_pts, LANES), jnp.bfloat16),
            pltpu.VMEM((rows_pts // 2, LANES), jnp.bfloat16),
            pltpu.VMEM((n_f, rows_dev, LANES), jnp.bfloat16),
            pltpu.VMEM((n_f, rows_dev // 2, LANES), jnp.bfloat16),
            pltpu.VMEM((1, LANES), jnp.float32),
            pltpu.VMEM((n, 1, LANES), jnp.float32),
            pltpu.VMEM((n_p, SUB, wide), jnp.float32),
            pltpu.VMEM((n_p, SUB, wide), jnp.float32),
            pltpu.VMEM((n_p, 1, LANES), jnp.float32),
            pltpu.VMEM((n, 1, LANES), jnp.float32),
            dma((tiles,)),
            dma((chunks, n_f - 1)), dma((chunks, n_f - 1)),
            dma((chunks, n_f - 1)), dma((chunks, n_f - 1)),
            dma((n - 1,)), dma((n - 1,)),
            dma((n_p - 1,)), dma((n_p - 1,)),
            dma((n - 1,)), dma((n - 1,)),
        ],
        compiler_params=pltpu.CompilerParams(
            collective_id=0, has_side_effects=True, vmem_limit_bytes=48 << 20
        ),
    )(slab, labels.reshape(1, -1), sample_rows, sample_count, slot_offset, centres)


def solution(mesh):
    n_p, n_f = mesh.shape["pts"], mesh.shape["feat"]

    def body(slab, centres, labels, sample_rows, sample_count, slot_offset):
        width = slab.shape[1]
        slots = sample_rows.shape[2]
        fits = (
            width == LANES + HALF and n_f % 2 == 0 and 3 * n_p * slots <= LANES
            and n_p * SUB <= LANES and 2 * slots <= SUB and centres.shape[0] % 512 == 0
            and slab.shape[0] % (n_f * 512) == 0
        )
        args = (slab, centres, labels, sample_rows, sample_count, slot_offset)
        return fused(n_p, n_f, *args) if fits else local(*args)

    placed = (
        P("pts", "feat"),
        P(),
        P(("pts", "feat"), None),
        P("pts", None, None),
        P("pts", None),
        P("pts", None),
    )
    return jax.shard_map(
        body, mesh=mesh, in_specs=placed, out_specs=P("pts", "feat"), check_vma=False
    )
```

```python
import functools

import jax
import jax.numpy as jnp
from jax import lax
from jax.experimental import pallas as pl
from jax.experimental.pallas import tpu as pltpu
from jax.sharding import PartitionSpec as P

NT = (((1,), (1,)), ((), ()))
LANES = 128
SUB = 8
CHUNK = 256
TILE = 512
MESH = pl.DeviceIdType.MESH


def local(slab, centres, labels, sample_rows, sample_count, slot_offset):
    rows_pts, feat_width = slab.shape
    feat_count = lax.axis_size("feat")
    rows_dev = rows_pts // feat_count
    centre_count = centres.shape[0]
    centre_sq = jnp.sum(jnp.square(centres.astype(jnp.float32)), axis=1)
    stacked = slab.reshape(feat_count, rows_dev, feat_width)
    points = lax.all_to_all(stacked, "feat", split_axis=0, concat_axis=2, tiled=True)[0]
    cross_term = lax.dot_general(points, centres, NT, preferred_element_type=jnp.float32)
    point_sq = jnp.sum(jnp.square(points.astype(jnp.float32)), axis=1)
    nearest = jnp.min(point_sq[:, None] + centre_sq[None, :] - 2.0 * cross_term, axis=1)[None, :][0]
    member = labels[:, 0]
    cost_part = jax.ops.segment_sum(nearest, member, num_segments=centre_count)
    size_part = jax.ops.segment_sum(jnp.ones_like(nearest), member, num_segments=centre_count)
    cluster_cost, cluster_size = lax.psum((cost_part, size_part), ("pts", "feat"))
    own_sens = nearest / jnp.take(cluster_cost, member) + 1.0 / jnp.take(cluster_size, member)
    shard_sens = lax.all_gather(own_sens, "feat", axis=0, tiled=True)
    total_points = rows_pts * lax.axis_size("pts")
    weight = 2.0 * centre_count / total_points / shard_sens
    picked_rows = sample_rows[0]
    owner_count, slot_count = picked_rows.shape
    chosen = jnp.take(slab, picked_rows.reshape(-1), axis=0).reshape(
        owner_count, slot_count, feat_width
    )
    chosen_weight = jnp.take(weight, picked_rows)
    live_slot = jnp.arange(slot_count, dtype=jnp.int32)[None, :] < sample_count[0][:, None]
    scaled = jnp.where(
        live_slot[:, :, None], chosen.astype(jnp.float32) * chosen_weight[:, :, None], 0.0
    ).astype(jnp.bfloat16)
    arrived = lax.all_to_all(scaled, "pts", split_axis=0, concat_axis=0, tiled=True)
    target = slot_offset[0][:, None] + jnp.arange(slot_count, dtype=jnp.int32)[None, :]
    own_rows = arrived.shape[0] * slot_count
    placed = jnp.zeros((own_rows, feat_width), jnp.float32)
    placed = placed.at[target.reshape(-1)].add(
        arrived.reshape(-1, feat_width).astype(jnp.float32), mode="drop"
    )
    return placed.astype(jnp.bfloat16)


def kernel(n_p, n_f, chunks, tile, slab_hbm, labels_hbm, rows_hbm, count_hbm, offset_hbm, cen_hbm,
           out_ref, cen, csq, slab_ref, points_ref, labels_ref, rows_ref, count_ref, offset_ref,
           lab_msg, lab_all, row_msg, row_all, red_msg, red_all, in_sem, cen_sem, a_send, a_recv,
           lab_send, lab_recv, row_send, row_recv, red_send, red_recv):
    f32, bf16 = jnp.float32, jnp.bfloat16
    width, rows_pts = slab_ref.shape
    rows_dev = rows_pts // n_f
    crow = rows_dev // chunks
    n = n_p * n_f
    centre_count = cen.shape[0]
    slots = rows_ref.shape[1]
    tiles = centre_count // tile
    my_p, my_f = lax.axis_index("pts"), lax.axis_index("feat")
    me = my_p * n_f + my_f

    def device(d):
        other = lax.rem(me + d, n)
        return other // n_f, lax.rem(other, n_f)

    barrier = pltpu.get_barrier_semaphore()
    for d in range(1, n):
        pl.semaphore_signal(barrier, inc=1, device_id=device(d), device_id_type=MESH)

    own_k = pl.ds(pl.multiple_of(my_f * width, width), width)
    own_cols = pl.ds(pl.multiple_of(my_f * rows_dev, rows_dev), rows_dev)
    in_copies = [
        pltpu.make_async_copy(rows_hbm, rows_ref, in_sem.at[0]),
        pltpu.make_async_copy(count_hbm, count_ref, in_sem.at[1]),
        pltpu.make_async_copy(offset_hbm, offset_ref, in_sem.at[2]),
        pltpu.make_async_copy(labels_hbm, labels_ref, in_sem.at[3]),
        pltpu.make_async_copy(slab_hbm, slab_ref, in_sem.at[4]),
        pltpu.make_async_copy(slab_hbm.at[:, own_cols], points_ref.at[own_k], in_sem.at[5]),
    ]
    for copy in in_copies:
        copy.start()
    cen_copies = []
    for t in range(tiles):
        part = pl.ds(t * tile, tile)
        copy = pltpu.make_async_copy(cen_hbm.at[part], cen.at[part], cen_sem.at[t])
        copy.start()
        cen_copies.append(copy)

    pl.semaphore_wait(barrier, n - 1)

    slab_copies = []
    order = [e for e in range(2, n_f)] + [1]
    for c in range(chunks):
        copies = []
        for e in order:
            peer = lax.rem(my_f + e, n_f)
            at = pl.multiple_of(peer * rows_dev + c * crow, crow)
            copies.append(pltpu.make_async_remote_copy(
                src_ref=slab_hbm.at[:, pl.ds(at, crow)],
                dst_ref=points_ref.at[own_k, pl.ds(c * crow, crow)],
                send_sem=a_send.at[c, e - 1], recv_sem=a_recv.at[c, e - 1],
                device_id=(my_p, peer), device_id_type=MESH))
        for copy in copies:
            copy.start()
        slab_copies.append(copies)
    for copy in in_copies:
        copy.wait()

    queries = n_p * SUB
    query_sub = lax.broadcasted_iota(jnp.int32, (queries, 1), 0)
    picked = jnp.full((queries, 1), -1, jnp.int32)
    for o in range(n_p):
        for s in range(slots):
            picked = jnp.where(query_sub == o * SUB + s, rows_ref[0, s, o], picked)
    members = labels_ref[...].astype(f32)
    lane_dev = lax.broadcasted_iota(jnp.int32, (queries, rows_dev), 1)
    own_hit = (lane_dev + my_f * rows_dev) == picked
    own_label = jnp.sum(jnp.where(own_hit, members + 1.0, 0.0), axis=1, keepdims=True)
    query_diag = (lax.broadcasted_iota(jnp.int32, (queries, LANES), 0)
                  == lax.broadcasted_iota(jnp.int32, (queries, LANES), 1))
    label_row = jnp.sum(jnp.where(query_diag, own_label, 0.0), axis=0, keepdims=True)
    lab_msg[...] = label_row
    lab_all[me] = label_row

    lab_copies = []
    for d in range(1, n):
        copy = pltpu.make_async_remote_copy(
            src_ref=lab_msg, dst_ref=lab_all.at[me], send_sem=lab_send.at[d - 1],
            recv_sem=lab_recv.at[d - 1], device_id=device(d), device_id_type=MESH)
        copy.start()
        lab_copies.append(copy)

    lane_pts = lax.broadcasted_iota(jnp.int32, (queries, rows_pts), 1)
    chosen = jnp.where(lane_pts == picked, 1.0, 0.0).astype(bf16)
    chosen = lax.dot_general(chosen, slab_ref[...], NT, preferred_element_type=f32)
    live = jnp.zeros((queries, 1), f32)
    for o in range(n_p):
        for s in range(slots):
            flag = jnp.where(count_ref[0, o] > s, 1.0, 0.0)
            live = jnp.where(query_sub == o * SUB + slots + s, flag, live)
    is_row = lax.rem(lax.broadcasted_iota(jnp.int32, (queries, width), 0), SUB) < slots
    sent = jnp.where(is_row, chosen, live)
    row_msg[:, :, :width] = sent.reshape(n_p, SUB, width)
    row_all[my_p] = row_msg[my_p]
    row_copies = []
    for d in range(1, n_p):
        owner = lax.rem(my_p + d, n_p)
        copy = pltpu.make_async_remote_copy(
            src_ref=row_msg.at[owner], dst_ref=row_all.at[my_p], send_sem=row_send.at[d - 1],
            recv_sem=row_recv.at[d - 1], device_id=(owner, my_f), device_id_type=MESH)
        copy.start()
        row_copies.append(copy)

    for t in range(tiles):
        cen_copies[t].wait()

    @pl.loop(0, tiles)
    def _(t):
        part = pl.ds(pl.multiple_of(t * tile, tile), tile)
        total = jnp.zeros((tile, LANES), f32)
        for b in range(cen.shape[1] // LANES):
            piece = cen[part, b * LANES:(b + 1) * LANES].astype(f32)
            total += piece * piece
        csq[part, :] = jnp.broadcast_to(jnp.sum(total, axis=1, keepdims=True), (tile, LANES))

    for copy in lab_copies:
        copy.wait()
    lanes = lax.broadcasted_iota(jnp.int32, (queries, LANES), 1)
    slot = lax.rem(lax.broadcasted_iota(jnp.int32, (queries, LANES), 0), SUB)
    is_slot = slot < slots
    wanted = []
    sums = jnp.zeros((queries, LANES), f32)
    span = n_p * slots
    for p in range(n_p):
        row = lab_all[p * n_f]
        for g in range(1, n_f):
            row = row + lab_all[p * n_f + g]
        want = jnp.sum(jnp.where(query_diag, row, 0.0), axis=1, keepdims=True) - 1.0
        wanted.append(want)
        size = jnp.sum(jnp.where(want == members, 1.0, 0.0), axis=1, keepdims=True)
        sums = jnp.where(is_slot & (lanes == span + p * slots + slot), size, sums)

    near_parts = []
    for c in range(chunks):
        for copy in slab_copies[c]:
            copy.wait_recv()
        points = points_ref[:, c * crow:(c + 1) * crow]
        wide = points.astype(f32)
        point_sq = jnp.sum(wide * wide, axis=0, keepdims=True)

        def step(t, best):
            part = pl.ds(pl.multiple_of(t * tile, tile), tile)
            cross = jnp.dot(cen[part, :], points, preferred_element_type=f32)
            square = csq[part, :]
            gap = jnp.concatenate([square] * (crow // LANES), axis=1) - 2.0 * cross
            return jnp.minimum(best, jnp.min(gap.reshape(tile // SUB, SUB, crow), axis=0))

        best = lax.fori_loop(0, tiles, step, jnp.full((SUB, crow), jnp.inf, f32))
        near_parts.append(point_sq + jnp.min(best, axis=0, keepdims=True))
    nearest = jnp.concatenate(near_parts, axis=1)

    for p in range(n_p):
        cost = jnp.sum(jnp.where(wanted[p] == members, nearest, 0.0), axis=1, keepdims=True)
        sums = jnp.where(is_slot & (lanes == p * slots + slot), cost, sums)
    own_near = jnp.sum(jnp.where(own_hit, nearest, 0.0), axis=1, keepdims=True)
    sums = jnp.where(is_slot & (lanes == 2 * span + my_p * slots + slot), own_near, sums)
    to_owner = jnp.sum(jnp.where(is_slot, sums, 0.0).reshape(n_p, SUB, LANES), axis=1, keepdims=True)
    red_msg[...] = to_owner
    red_all[0] = red_msg[my_p]
    red_copies = []
    for d in range(1, n):
        to = device(d)
        copy = pltpu.make_async_remote_copy(
            src_ref=red_msg.at[to[0]], dst_ref=red_all.at[d], send_sem=red_send.at[d - 1],
            recv_sem=red_recv.at[d - 1], device_id=to, device_id_type=MESH)
        copy.start()
        red_copies.append(copy)
    for copy in row_copies:
        copy.wait()
    for copies in slab_copies:
        for copy in copies:
            copy.wait_send()
    for copy in red_copies:
        copy.wait()
    total = jnp.broadcast_to(jnp.sum(red_all[...], axis=0), (SUB, LANES))
    size = pltpu.roll(total, LANES - span, 1)
    near = pltpu.roll(total, LANES - 2 * span, 1)
    weight = (2.0 * centre_count / (rows_pts * n_p)) / (near / total + 1.0 / size)
    sub = lax.broadcasted_iota(jnp.int32, (SUB, LANES), 0)
    lane = lax.broadcasted_iota(jnp.int32, (SUB, LANES), 1)
    out_rows = out_ref.shape[0]
    out_iota = lax.broadcasted_iota(jnp.int32, (out_rows, width), 0)
    placed = jnp.zeros((out_rows, width), f32)
    for p in range(n_p):
        mine = (sub < slots) & (lane == p * slots + sub)
        factor = jnp.sum(jnp.where(mine, weight, 0.0), axis=1, keepdims=True)
        block = row_all[p][:, :width]
        scaled = (block * factor).astype(bf16).astype(f32)
        for s in range(slots):
            flag = block[slots + s:slots + s + 1] > 0.5
            hit = (out_iota == offset_ref[0, p] + s) & flag
            placed = jnp.where(hit, scaled[s:s + 1], placed)
    out_ref[...] = placed.astype(bf16)


def fused(n_p, n_f, slab, centres, labels, sample_rows, sample_count, slot_offset):
    rows_pts, width = slab.shape
    rows_dev = rows_pts // n_f
    centre_count, depth = centres.shape
    slots = sample_rows.shape[2]
    chunks = rows_dev // CHUNK
    tiles = centre_count // TILE
    n = n_p * n_f
    wide = pl.cdiv(width, LANES) * LANES
    rows_in = sample_rows.transpose(0, 2, 1)
    labels_in = labels.reshape(1, -1)
    dma = pltpu.SemaphoreType.DMA
    return pl.pallas_call(
        functools.partial(kernel, n_p, n_f, chunks, TILE),
        out_shape=jax.ShapeDtypeStruct((n_p * slots, width), jnp.bfloat16),
        in_specs=[pl.BlockSpec(memory_space=pl.ANY)] * 6,
        out_specs=pl.BlockSpec(memory_space=pltpu.VMEM),
        scratch_shapes=[
            pltpu.VMEM((centre_count, depth), jnp.bfloat16),
            pltpu.VMEM((centre_count, LANES), jnp.float32),
            pltpu.VMEM((width, rows_pts), jnp.bfloat16),
            pltpu.VMEM((depth, rows_dev), jnp.bfloat16),
            pltpu.VMEM(labels_in.shape, jnp.int32),
            pltpu.SMEM(rows_in.shape, jnp.int32),
            pltpu.SMEM(sample_count.shape, jnp.int32),
            pltpu.SMEM(slot_offset.shape, jnp.int32),
            pltpu.VMEM((1, LANES), jnp.float32),
            pltpu.VMEM((n, 1, LANES), jnp.float32),
            pltpu.VMEM((n_p, SUB, wide), jnp.float32),
            pltpu.VMEM((n_p, SUB, wide), jnp.float32),
            pltpu.VMEM((n_p, 1, LANES), jnp.float32),
            pltpu.VMEM((n, 1, LANES), jnp.float32),
            dma((6,)), dma((tiles,)),
            dma((chunks, n_f - 1)), dma((chunks, n_f - 1)),
            dma((n - 1,)), dma((n - 1,)),
            dma((n_p - 1,)), dma((n_p - 1,)),
            dma((n - 1,)), dma((n - 1,)),
        ],
        compiler_params=pltpu.CompilerParams(collective_id=0, has_side_effects=True),
    )(slab.T, labels_in, rows_in, sample_count, slot_offset, centres)


def solution(mesh):
    n_p, n_f = mesh.shape["pts"], mesh.shape["feat"]

    def body(slab, centres, labels, sample_rows, sample_count, slot_offset):
        rows_dev = slab.shape[0] // n_f
        slots = sample_rows.shape[2]
        fits = (
            slab.shape[1] % 16 == 0 and rows_dev % CHUNK == 0 and centres.shape[0] % TILE == 0
            and 3 * n_p * slots <= LANES and n_p * SUB <= LANES and 2 * slots <= SUB
        )
        args = (slab, centres, labels, sample_rows, sample_count, slot_offset)
        return fused(n_p, n_f, *args) if fits else local(*args)

    placed = (
        P("pts", "feat"),
        P(),
        P(("pts", "feat"), None),
        P("pts", None, None),
        P("pts", None),
        P("pts", None),
    )
    return jax.shard_map(
        body, mesh=mesh, in_specs=placed, out_specs=P("pts", "feat"), check_vma=False
    )
```

```python
import functools

import jax
import jax.numpy as jnp
from jax import lax
from jax.experimental import pallas as pl
from jax.experimental.pallas import tpu as pltpu
from jax.sharding import PartitionSpec as P

NT = (((1,), (1,)), ((), ()))
LANES = 128
SUB = 8
CHUNK = 256
TILE = 512
MESH = pl.DeviceIdType.MESH


def local(slab, centres, labels, sample_rows, sample_count, slot_offset):
    rows_pts, feat_width = slab.shape
    feat_count = lax.axis_size("feat")
    rows_dev = rows_pts // feat_count
    centre_count = centres.shape[0]
    centre_sq = jnp.sum(jnp.square(centres.astype(jnp.float32)), axis=1)
    stacked = slab.reshape(feat_count, rows_dev, feat_width)
    points = lax.all_to_all(stacked, "feat", split_axis=0, concat_axis=2, tiled=True)[0]
    cross_term = lax.dot_general(points, centres, NT, preferred_element_type=jnp.float32)
    point_sq = jnp.sum(jnp.square(points.astype(jnp.float32)), axis=1)
    nearest = jnp.min(point_sq[:, None] + centre_sq[None, :] - 2.0 * cross_term, axis=1)[None, :][0]
    member = labels[:, 0]
    cost_part = jax.ops.segment_sum(nearest, member, num_segments=centre_count)
    size_part = jax.ops.segment_sum(jnp.ones_like(nearest), member, num_segments=centre_count)
    cluster_cost, cluster_size = lax.psum((cost_part, size_part), ("pts", "feat"))
    own_sens = nearest / jnp.take(cluster_cost, member) + 1.0 / jnp.take(cluster_size, member)
    shard_sens = lax.all_gather(own_sens, "feat", axis=0, tiled=True)
    total_points = rows_pts * lax.axis_size("pts")
    weight = 2.0 * centre_count / total_points / shard_sens
    picked_rows = sample_rows[0]
    owner_count, slot_count = picked_rows.shape
    chosen = jnp.take(slab, picked_rows.reshape(-1), axis=0).reshape(
        owner_count, slot_count, feat_width
    )
    chosen_weight = jnp.take(weight, picked_rows)
    live_slot = jnp.arange(slot_count, dtype=jnp.int32)[None, :] < sample_count[0][:, None]
    scaled = jnp.where(
        live_slot[:, :, None], chosen.astype(jnp.float32) * chosen_weight[:, :, None], 0.0
    ).astype(jnp.bfloat16)
    arrived = lax.all_to_all(scaled, "pts", split_axis=0, concat_axis=0, tiled=True)
    target = slot_offset[0][:, None] + jnp.arange(slot_count, dtype=jnp.int32)[None, :]
    own_rows = arrived.shape[0] * slot_count
    placed = jnp.zeros((own_rows, feat_width), jnp.float32)
    placed = placed.at[target.reshape(-1)].add(
        arrived.reshape(-1, feat_width).astype(jnp.float32), mode="drop"
    )
    return placed.astype(jnp.bfloat16)


def kernel(n_p, n_f, chunks, tile, slab_hbm, labels_hbm, rows_hbm, count_hbm, offset_hbm, cen_hbm,
           out_ref, cen, csq, slab_ref, points_ref, labels_ref, rows_ref, count_ref, offset_ref,
           lab_msg, lab_all, row_msg, row_all, red_msg, red_all, in_sem, cen_sem, a_send, a_recv,
           lab_send, lab_recv, row_send, row_recv, red_send, red_recv):
    f32, bf16 = jnp.float32, jnp.bfloat16
    width, rows_pts = slab_ref.shape
    rows_dev = rows_pts // n_f
    crow = rows_dev // chunks
    n = n_p * n_f
    centre_count = cen.shape[0]
    slots = rows_ref.shape[1]
    tiles = centre_count // tile
    my_p, my_f = lax.axis_index("pts"), lax.axis_index("feat")
    me = my_p * n_f + my_f

    def device(d):
        other = lax.rem(me + d, n)
        return other // n_f, lax.rem(other, n_f)

    barrier = pltpu.get_barrier_semaphore()
    for d in range(1, n):
        pl.semaphore_signal(barrier, inc=1, device_id=device(d), device_id_type=MESH)

    own_k = pl.ds(pl.multiple_of(my_f * width, width), width)
    own_cols = pl.ds(pl.multiple_of(my_f * rows_dev, rows_dev), rows_dev)
    in_copies = [
        pltpu.make_async_copy(rows_hbm, rows_ref, in_sem.at[0]),
        pltpu.make_async_copy(count_hbm, count_ref, in_sem.at[1]),
        pltpu.make_async_copy(offset_hbm, offset_ref, in_sem.at[2]),
        pltpu.make_async_copy(labels_hbm, labels_ref, in_sem.at[3]),
        pltpu.make_async_copy(slab_hbm, slab_ref, in_sem.at[4]),
        pltpu.make_async_copy(slab_hbm.at[:, own_cols], points_ref.at[own_k], in_sem.at[5]),
    ]
    for copy in in_copies:
        copy.start()
    cen_copies = []
    for t in range(tiles):
        part = pl.ds(t * tile, tile)
        copy = pltpu.make_async_copy(cen_hbm.at[part], cen.at[part], cen_sem.at[t])
        copy.start()
        cen_copies.append(copy)

    for copy in in_copies[:4]:
        copy.wait()

    queries = n_p * SUB
    query_sub = lax.broadcasted_iota(jnp.int32, (queries, 1), 0)
    picked = jnp.full((queries, 1), -1, jnp.int32)
    for o in range(n_p):
        for s in range(slots):
            picked = jnp.where(query_sub == o * SUB + s, rows_ref[0, s, o], picked)
    members = labels_ref[...].astype(f32)
    lane_dev = lax.broadcasted_iota(jnp.int32, (queries, rows_dev), 1)
    own_hit = (lane_dev + my_f * rows_dev) == picked
    own_label = jnp.sum(jnp.where(own_hit, members + 1.0, 0.0), axis=1, keepdims=True)
    query_diag = (lax.broadcasted_iota(jnp.int32, (queries, LANES), 0)
                  == lax.broadcasted_iota(jnp.int32, (queries, LANES), 1))
    label_row = jnp.sum(jnp.where(query_diag, own_label, 0.0), axis=0, keepdims=True)
    lab_msg[...] = label_row
    lab_all[me] = label_row

    pl.semaphore_wait(barrier, n - 1)

    lab_copies = []
    for d in range(1, n):
        copy = pltpu.make_async_remote_copy(
            src_ref=lab_msg, dst_ref=lab_all.at[me], send_sem=lab_send.at[d - 1],
            recv_sem=lab_recv.at[d - 1], device_id=device(d), device_id_type=MESH)
        copy.start()
        lab_copies.append(copy)

    slab_copies = []
    order = [e for e in range(2, n_f)] + [1]
    for c in range(chunks):
        copies = []
        for e in order:
            peer = lax.rem(my_f + e, n_f)
            at = pl.multiple_of(peer * rows_dev + c * crow, crow)
            copies.append(pltpu.make_async_remote_copy(
                src_ref=slab_hbm.at[:, pl.ds(at, crow)],
                dst_ref=points_ref.at[own_k, pl.ds(c * crow, crow)],
                send_sem=a_send.at[c, e - 1], recv_sem=a_recv.at[c, e - 1],
                device_id=(my_p, peer), device_id_type=MESH))
        for copy in copies:
            copy.start()
        slab_copies.append(copies)
    for copy in in_copies[4:]:
        copy.wait()

    lane_pts = lax.broadcasted_iota(jnp.int32, (queries, rows_pts), 1)
    chosen = jnp.where(lane_pts == picked, 1.0, 0.0).astype(bf16)
    chosen = lax.dot_general(chosen, slab_ref[...], NT, preferred_element_type=f32)
    live = jnp.zeros((queries, 1), f32)
    for o in range(n_p):
        for s in range(slots):
            flag = jnp.where(count_ref[0, o] > s, 1.0, 0.0)
            live = jnp.where(query_sub == o * SUB + slots + s, flag, live)
    is_row = lax.rem(lax.broadcasted_iota(jnp.int32, (queries, width), 0), SUB) < slots
    sent = jnp.where(is_row, chosen, live)
    row_msg[:, :, :width] = sent.reshape(n_p, SUB, width)
    row_all[my_p] = row_msg[my_p]
    row_copies = []
    for d in range(1, n_p):
        owner = lax.rem(my_p + d, n_p)
        copy = pltpu.make_async_remote_copy(
            src_ref=row_msg.at[owner], dst_ref=row_all.at[my_p], send_sem=row_send.at[d - 1],
            recv_sem=row_recv.at[d - 1], device_id=(owner, my_f), device_id_type=MESH)
        copy.start()
        row_copies.append(copy)

    for t in range(tiles):
        cen_copies[t].wait()

    @pl.loop(0, tiles)
    def _(t):
        part = pl.ds(pl.multiple_of(t * tile, tile), tile)
        total = jnp.zeros((tile, LANES), f32)
        for b in range(cen.shape[1] // LANES):
            piece = cen[part, b * LANES:(b + 1) * LANES].astype(f32)
            total += piece * piece
        csq[part, :] = jnp.broadcast_to(jnp.sum(total, axis=1, keepdims=True), (tile, LANES))

    for copy in lab_copies:
        copy.wait()
    lanes = lax.broadcasted_iota(jnp.int32, (queries, LANES), 1)
    slot = lax.rem(lax.broadcasted_iota(jnp.int32, (queries, LANES), 0), SUB)
    is_slot = slot < slots
    wanted = []
    sums = jnp.zeros((queries, LANES), f32)
    span = n_p * slots
    for p in range(n_p):
        row = lab_all[p * n_f]
        for g in range(1, n_f):
            row = row + lab_all[p * n_f + g]
        want = jnp.sum(jnp.where(query_diag, row, 0.0), axis=1, keepdims=True) - 1.0
        wanted.append(want)
        size = jnp.sum(jnp.where(want == members, 1.0, 0.0), axis=1, keepdims=True)
        sums = jnp.where(is_slot & (lanes == span + p * slots + slot), size, sums)

    near_parts = []
    for c in range(chunks):
        for copy in slab_copies[c]:
            copy.wait_recv()
        points = points_ref[:, c * crow:(c + 1) * crow]
        wide = points.astype(f32)
        point_sq = jnp.sum(wide * wide, axis=0, keepdims=True)

        def step(t, best):
            part = pl.ds(pl.multiple_of(t * tile, tile), tile)
            cross = jnp.dot(cen[part, :], points, preferred_element_type=f32)
            square = csq[part, :]
            gap = jnp.concatenate([square] * (crow // LANES), axis=1) - 2.0 * cross
            return jnp.minimum(best, jnp.min(gap.reshape(tile // SUB, SUB, crow), axis=0))

        best = lax.fori_loop(0, tiles, step, jnp.full((SUB, crow), jnp.inf, f32))
        near_parts.append(point_sq + jnp.min(best, axis=0, keepdims=True))
    nearest = jnp.concatenate(near_parts, axis=1)

    for p in range(n_p):
        cost = jnp.sum(jnp.where(wanted[p] == members, nearest, 0.0), axis=1, keepdims=True)
        sums = jnp.where(is_slot & (lanes == p * slots + slot), cost, sums)
    own_near = jnp.sum(jnp.where(own_hit, nearest, 0.0), axis=1, keepdims=True)
    sums = jnp.where(is_slot & (lanes == 2 * span + my_p * slots + slot), own_near, sums)
    to_owner = jnp.sum(jnp.where(is_slot, sums, 0.0).reshape(n_p, SUB, LANES), axis=1, keepdims=True)
    red_msg[...] = to_owner
    red_all[0] = red_msg[my_p]
    red_copies = []
    for d in range(1, n):
        to = device(d)
        copy = pltpu.make_async_remote_copy(
            src_ref=red_msg.at[to[0]], dst_ref=red_all.at[d], send_sem=red_send.at[d - 1],
            recv_sem=red_recv.at[d - 1], device_id=to, device_id_type=MESH)
        copy.start()
        red_copies.append(copy)
    for copy in row_copies:
        copy.wait()
    for copies in slab_copies:
        for copy in copies:
            copy.wait_send()
    for copy in red_copies:
        copy.wait()
    total = jnp.broadcast_to(jnp.sum(red_all[...], axis=0), (SUB, LANES))
    size = pltpu.roll(total, LANES - span, 1)
    near = pltpu.roll(total, LANES - 2 * span, 1)
    weight = (2.0 * centre_count / (rows_pts * n_p)) / (near / total + 1.0 / size)
    sub = lax.broadcasted_iota(jnp.int32, (SUB, LANES), 0)
    lane = lax.broadcasted_iota(jnp.int32, (SUB, LANES), 1)
    out_rows = out_ref.shape[0]
    out_iota = lax.broadcasted_iota(jnp.int32, (out_rows, width), 0)
    placed = jnp.zeros((out_rows, width), f32)
    for p in range(n_p):
        mine = (sub < slots) & (lane == p * slots + sub)
        factor = jnp.sum(jnp.where(mine, weight, 0.0), axis=1, keepdims=True)
        block = row_all[p][:, :width]
        scaled = (block * factor).astype(bf16).astype(f32)
        for s in range(slots):
            flag = block[slots + s:slots + s + 1] > 0.5
            hit = (out_iota == offset_ref[0, p] + s) & flag
            placed = jnp.where(hit, scaled[s:s + 1], placed)
    out_ref[...] = placed.astype(bf16)


def fused(n_p, n_f, slab, centres, labels, sample_rows, sample_count, slot_offset):
    rows_pts, width = slab.shape
    rows_dev = rows_pts // n_f
    centre_count, depth = centres.shape
    slots = sample_rows.shape[2]
    chunks = rows_dev // CHUNK
    tiles = centre_count // TILE
    n = n_p * n_f
    wide = pl.cdiv(width, LANES) * LANES
    rows_in = sample_rows.transpose(0, 2, 1)
    labels_in = labels.reshape(1, -1)
    dma = pltpu.SemaphoreType.DMA
    return pl.pallas_call(
        functools.partial(kernel, n_p, n_f, chunks, TILE),
        out_shape=jax.ShapeDtypeStruct((n_p * slots, width), jnp.bfloat16),
        in_specs=[pl.BlockSpec(memory_space=pl.ANY)] * 6,
        out_specs=pl.BlockSpec(memory_space=pltpu.VMEM),
        scratch_shapes=[
            pltpu.VMEM((centre_count, depth), jnp.bfloat16),
            pltpu.VMEM((centre_count, LANES), jnp.float32),
            pltpu.VMEM((width, rows_pts), jnp.bfloat16),
            pltpu.VMEM((depth, rows_dev), jnp.bfloat16),
            pltpu.VMEM(labels_in.shape, jnp.int32),
            pltpu.SMEM(rows_in.shape, jnp.int32),
            pltpu.SMEM(sample_count.shape, jnp.int32),
            pltpu.SMEM(slot_offset.shape, jnp.int32),
            pltpu.VMEM((1, LANES), jnp.float32),
            pltpu.VMEM((n, 1, LANES), jnp.float32),
            pltpu.VMEM((n_p, SUB, wide), jnp.float32),
            pltpu.VMEM((n_p, SUB, wide), jnp.float32),
            pltpu.VMEM((n_p, 1, LANES), jnp.float32),
            pltpu.VMEM((n, 1, LANES), jnp.float32),
            dma((6,)), dma((tiles,)),
            dma((chunks, n_f - 1)), dma((chunks, n_f - 1)),
            dma((n - 1,)), dma((n - 1,)),
            dma((n_p - 1,)), dma((n_p - 1,)),
            dma((n - 1,)), dma((n - 1,)),
        ],
        compiler_params=pltpu.CompilerParams(collective_id=0, has_side_effects=True),
    )(slab.T, labels_in, rows_in, sample_count, slot_offset, centres)


def solution(mesh):
    n_p, n_f = mesh.shape["pts"], mesh.shape["feat"]

    def body(slab, centres, labels, sample_rows, sample_count, slot_offset):
        rows_dev = slab.shape[0] // n_f
        slots = sample_rows.shape[2]
        fits = (
            slab.shape[1] % 16 == 0 and rows_dev % CHUNK == 0 and centres.shape[0] % TILE == 0
            and 3 * n_p * slots <= LANES and n_p * SUB <= LANES and 2 * slots <= SUB
        )
        args = (slab, centres, labels, sample_rows, sample_count, slot_offset)
        return fused(n_p, n_f, *args) if fits else local(*args)

    placed = (
        P("pts", "feat"),
        P(),
        P(("pts", "feat"), None),
        P("pts", None, None),
        P("pts", None),
        P("pts", None),
    )
    return jax.shard_map(
        body, mesh=mesh, in_specs=placed, out_specs=P("pts", "feat"), check_vma=False
    )
```

```python
import functools

import jax
import jax.numpy as jnp
from jax import lax
from jax.experimental import pallas as pl
from jax.experimental.pallas import tpu as pltpu
from jax.sharding import PartitionSpec as P

NT = (((1,), (1,)), ((), ()))
LANES = 128
SUB = 8
CHUNK = 256
TILE = 2048
MESH = pl.DeviceIdType.MESH


def local(slab, centres, labels, sample_rows, sample_count, slot_offset):
    rows_pts, feat_width = slab.shape
    feat_count = lax.axis_size("feat")
    rows_dev = rows_pts // feat_count
    centre_count = centres.shape[0]
    centre_sq = jnp.sum(jnp.square(centres.astype(jnp.float32)), axis=1)
    stacked = slab.reshape(feat_count, rows_dev, feat_width)
    points = lax.all_to_all(stacked, "feat", split_axis=0, concat_axis=2, tiled=True)[0]
    cross_term = lax.dot_general(points, centres, NT, preferred_element_type=jnp.float32)
    point_sq = jnp.sum(jnp.square(points.astype(jnp.float32)), axis=1)
    nearest = jnp.min(point_sq[:, None] + centre_sq[None, :] - 2.0 * cross_term, axis=1)[None, :][0]
    member = labels[:, 0]
    cost_part = jax.ops.segment_sum(nearest, member, num_segments=centre_count)
    size_part = jax.ops.segment_sum(jnp.ones_like(nearest), member, num_segments=centre_count)
    cluster_cost, cluster_size = lax.psum((cost_part, size_part), ("pts", "feat"))
    own_sens = nearest / jnp.take(cluster_cost, member) + 1.0 / jnp.take(cluster_size, member)
    shard_sens = lax.all_gather(own_sens, "feat", axis=0, tiled=True)
    total_points = rows_pts * lax.axis_size("pts")
    weight = 2.0 * centre_count / total_points / shard_sens
    picked_rows = sample_rows[0]
    owner_count, slot_count = picked_rows.shape
    chosen = jnp.take(slab, picked_rows.reshape(-1), axis=0).reshape(
        owner_count, slot_count, feat_width
    )
    chosen_weight = jnp.take(weight, picked_rows)
    live_slot = jnp.arange(slot_count, dtype=jnp.int32)[None, :] < sample_count[0][:, None]
    scaled = jnp.where(
        live_slot[:, :, None], chosen.astype(jnp.float32) * chosen_weight[:, :, None], 0.0
    ).astype(jnp.bfloat16)
    arrived = lax.all_to_all(scaled, "pts", split_axis=0, concat_axis=0, tiled=True)
    target = slot_offset[0][:, None] + jnp.arange(slot_count, dtype=jnp.int32)[None, :]
    own_rows = arrived.shape[0] * slot_count
    placed = jnp.zeros((own_rows, feat_width), jnp.float32)
    placed = placed.at[target.reshape(-1)].add(
        arrived.reshape(-1, feat_width).astype(jnp.float32), mode="drop"
    )
    return placed.astype(jnp.bfloat16)


def kernel(n_p, n_f, chunks, tile, slab_hbm, labels_hbm, rows_hbm, count_hbm, offset_hbm, cen_hbm,
           out_ref, cen, csq, gap_ref, slab_ref, points_ref, labels_ref, rows_ref, count_ref, offset_ref,
           lab_msg, lab_all, row_msg, row_all, red_msg, red_all, in_sem, cen_sem, a_send, a_recv,
           lab_send, lab_recv, row_send, row_recv, red_send, red_recv):
    f32, bf16 = jnp.float32, jnp.bfloat16
    width, rows_pts = slab_ref.shape
    rows_dev = rows_pts // n_f
    crow = rows_dev // chunks
    n = n_p * n_f
    centre_count = cen.shape[0]
    slots = rows_ref.shape[1]
    tiles = centre_count // tile
    my_p, my_f = lax.axis_index("pts"), lax.axis_index("feat")
    me = my_p * n_f + my_f

    def device(d):
        other = lax.rem(me + d, n)
        return other // n_f, lax.rem(other, n_f)

    barrier = pltpu.get_barrier_semaphore()
    for d in range(1, n):
        pl.semaphore_signal(barrier, inc=1, device_id=device(d), device_id_type=MESH)

    own_k = pl.ds(pl.multiple_of(my_f * width, width), width)
    own_cols = pl.ds(pl.multiple_of(my_f * rows_dev, rows_dev), rows_dev)
    in_copies = [
        pltpu.make_async_copy(rows_hbm, rows_ref, in_sem.at[0]),
        pltpu.make_async_copy(count_hbm, count_ref, in_sem.at[1]),
        pltpu.make_async_copy(offset_hbm, offset_ref, in_sem.at[2]),
        pltpu.make_async_copy(labels_hbm, labels_ref, in_sem.at[3]),
        pltpu.make_async_copy(slab_hbm, slab_ref, in_sem.at[4]),
        pltpu.make_async_copy(slab_hbm.at[:, own_cols], points_ref.at[own_k], in_sem.at[5]),
    ]
    for copy in in_copies:
        copy.start()
    cen_copies = []
    for t in range(tiles):
        part = pl.ds(t * tile, tile)
        copy = pltpu.make_async_copy(cen_hbm.at[part], cen.at[part], cen_sem.at[t])
        copy.start()
        cen_copies.append(copy)

    pl.semaphore_wait(barrier, n - 1)

    odd = lax.rem(my_f, 2)
    partner = my_f + 1 - 2 * odd
    peers = [partner, lax.rem(my_f + 2, n_f), lax.rem(partner + 2, n_f)]
    slab_copies = []
    for c in range(chunks):
        copies = []
        for r, peer in enumerate(peers):
            at = pl.multiple_of(peer * rows_dev + c * crow, crow)
            copies.append(pltpu.make_async_remote_copy(
                src_ref=slab_hbm.at[:, pl.ds(at, crow)],
                dst_ref=points_ref.at[own_k, pl.ds(c * crow, crow)],
                send_sem=a_send.at[c, r], recv_sem=a_recv.at[c, r],
                device_id=(my_p, peer), device_id_type=MESH))
        slab_copies.append(copies)
    for copy in slab_copies[0][1:] + slab_copies[0][:1]:
        copy.start()

    for copy in in_copies[:4]:
        copy.wait()

    queries = n_p * SUB
    query_sub = lax.broadcasted_iota(jnp.int32, (queries, 1), 0)
    picked = jnp.full((queries, 1), -1, jnp.int32)
    for o in range(n_p):
        for s in range(slots):
            picked = jnp.where(query_sub == o * SUB + s, rows_ref[0, s, o], picked)
    members = labels_ref[...].astype(f32)
    lane_dev = lax.broadcasted_iota(jnp.int32, (queries, rows_dev), 1)
    own_hit = (lane_dev + my_f * rows_dev) == picked
    own_label = jnp.sum(jnp.where(own_hit, members + 1.0, 0.0), axis=1, keepdims=True)
    query_diag = (lax.broadcasted_iota(jnp.int32, (queries, LANES), 0)
                  == lax.broadcasted_iota(jnp.int32, (queries, LANES), 1))
    label_row = jnp.sum(jnp.where(query_diag, own_label, 0.0), axis=0, keepdims=True)
    lab_msg[...] = label_row
    lab_all[me] = label_row


    lab_copies = []
    for d in range(1, n):
        copy = pltpu.make_async_remote_copy(
            src_ref=lab_msg, dst_ref=lab_all.at[me], send_sem=lab_send.at[d - 1],
            recv_sem=lab_recv.at[d - 1], device_id=device(d), device_id_type=MESH)
        copy.start()
        lab_copies.append(copy)

    for copies in slab_copies[1:]:
        for copy in copies[1:] + copies[:1]:
            copy.start()
    for copy in in_copies[4:]:
        copy.wait()

    lane_pts = lax.broadcasted_iota(jnp.int32, (queries, rows_pts), 1)
    chosen = jnp.where(lane_pts == picked, 1.0, 0.0).astype(bf16)
    chosen = lax.dot_general(chosen, slab_ref[...], NT, preferred_element_type=f32)
    live = jnp.zeros((queries, 1), f32)
    for o in range(n_p):
        for s in range(slots):
            flag = jnp.where(count_ref[0, o] > s, 1.0, 0.0)
            live = jnp.where(query_sub == o * SUB + slots + s, flag, live)
    is_row = lax.rem(lax.broadcasted_iota(jnp.int32, (queries, width), 0), SUB) < slots
    sent = jnp.where(is_row, chosen, live)
    row_msg[:, :, :width] = sent.reshape(n_p, SUB, width)
    row_all[my_p] = row_msg[my_p]
    row_copies = []
    for d in range(1, n_p):
        owner = lax.rem(my_p + d, n_p)
        copy = pltpu.make_async_remote_copy(
            src_ref=row_msg.at[owner], dst_ref=row_all.at[my_p], send_sem=row_send.at[d - 1],
            recv_sem=row_recv.at[d - 1], device_id=(owner, my_f), device_id_type=MESH)
        copy.start()
        row_copies.append(copy)

    for t in range(tiles):
        cen_copies[t].wait()

    @pl.loop(0, tiles)
    def _(t):
        part = pl.ds(pl.multiple_of(t * tile, tile), tile)
        total = jnp.zeros((tile, LANES), f32)
        for b in range(cen.shape[1] // LANES):
            piece = cen[part, b * LANES:(b + 1) * LANES].astype(f32)
            total += piece * piece
        csq[part, :] = jnp.broadcast_to(jnp.sum(total, axis=1, keepdims=True), (tile, LANES))

    start = jnp.full((SUB, crow), jnp.inf, f32)

    def part_of(t):
        return pl.ds(pl.multiple_of(t * tile, tile), tile)

    def lower(best, gap):
        return jnp.minimum(best, jnp.min(gap.reshape(tile // SUB, SUB, crow), axis=0))

    def squares(part):
        return jnp.concatenate([csq[part, :]] * (crow // LANES), axis=1)

    def finish(best, cols):
        wide = points_ref[:, cols].astype(f32)
        return jnp.sum(wide * wide, axis=0, keepdims=True) + jnp.min(best, axis=0, keepdims=True)

    near_parts = []
    for c in range(chunks - 1):
        for copy in slab_copies[c]:
            copy.wait_recv()
        cols = pl.ds(c * crow, crow)
        points = points_ref[:, cols]

        def step(t, best):
            part = part_of(t)
            cross = jnp.dot(cen[part, :], points, preferred_element_type=f32)
            return lower(best, squares(part) - 2.0 * cross)

        near_parts.append(finish(lax.fori_loop(0, tiles, step, start), cols))

    for copy in lab_copies:
        copy.wait()
    lanes = lax.broadcasted_iota(jnp.int32, (queries, LANES), 1)
    slot = lax.rem(lax.broadcasted_iota(jnp.int32, (queries, LANES), 0), SUB)
    is_slot = slot < slots
    wanted = []
    sums = jnp.zeros((queries, LANES), f32)
    span = n_p * slots
    for p in range(n_p):
        row = lab_all[p * n_f]
        for g in range(1, n_f):
            row = row + lab_all[p * n_f + g]
        want = jnp.sum(jnp.where(query_diag, row, 0.0), axis=1, keepdims=True) - 1.0
        wanted.append(want)
        size = jnp.sum(jnp.where(want == members, 1.0, 0.0), axis=1, keepdims=True)
        sums = jnp.where(is_slot & (lanes == span + p * slots + slot), size, sums)

    pair = 2 * width
    last = pl.cdiv(width, LANES) * LANES
    here = my_f // 2
    away = 1 - here
    cols = pl.ds((chunks - 1) * crow, crow)
    here_k = pl.ds(pl.multiple_of(here * pair, LANES), pair)
    lone_k = pl.ds(pl.multiple_of(away * pair + odd * last, LANES), pair - last)
    last_k = pl.ds(pl.multiple_of(away * pair + (1 - odd) * (pair - last), LANES), last)
    for copy in slab_copies[-1][:2]:
        copy.wait_recv()
    first = jnp.concatenate([points_ref[here_k, cols], points_ref[lone_k, cols]], axis=0)

    @pl.loop(0, tiles)
    def _(t):
        part = part_of(t)
        mine = jnp.concatenate([cen[part, here_k], cen[part, lone_k]], axis=1)
        cross = jnp.dot(mine, first, preferred_element_type=f32)
        gap_ref[part, :] = squares(part) - 2.0 * cross

    slab_copies[-1][2].wait_recv()
    final = points_ref[last_k, cols]

    def last_step(t, best):
        part = part_of(t)
        cross = jnp.dot(cen[part, last_k], final, preferred_element_type=f32)
        return lower(best, gap_ref[part, :] - 2.0 * cross)

    near_parts.append(finish(lax.fori_loop(0, tiles, last_step, start), cols))
    nearest = jnp.concatenate(near_parts, axis=1)

    for p in range(n_p):
        cost = jnp.sum(jnp.where(wanted[p] == members, nearest, 0.0), axis=1, keepdims=True)
        sums = jnp.where(is_slot & (lanes == p * slots + slot), cost, sums)
    own_near = jnp.sum(jnp.where(own_hit, nearest, 0.0), axis=1, keepdims=True)
    sums = jnp.where(is_slot & (lanes == 2 * span + my_p * slots + slot), own_near, sums)
    to_owner = jnp.sum(jnp.where(is_slot, sums, 0.0).reshape(n_p, SUB, LANES), axis=1, keepdims=True)
    red_msg[...] = to_owner
    red_all[0] = red_msg[my_p]
    red_copies = []
    for d in range(1, n):
        to = device(d)
        copy = pltpu.make_async_remote_copy(
            src_ref=red_msg.at[to[0]], dst_ref=red_all.at[d], send_sem=red_send.at[d - 1],
            recv_sem=red_recv.at[d - 1], device_id=to, device_id_type=MESH)
        copy.start()
        red_copies.append(copy)
    for copy in row_copies:
        copy.wait()
    for copies in slab_copies:
        for copy in copies:
            copy.wait_send()
    for copy in red_copies:
        copy.wait()
    total = jnp.broadcast_to(jnp.sum(red_all[...], axis=0), (SUB, LANES))
    size = pltpu.roll(total, LANES - span, 1)
    near = pltpu.roll(total, LANES - 2 * span, 1)
    weight = (2.0 * centre_count / (rows_pts * n_p)) / (near / total + 1.0 / size)
    sub = lax.broadcasted_iota(jnp.int32, (SUB, LANES), 0)
    lane = lax.broadcasted_iota(jnp.int32, (SUB, LANES), 1)
    out_rows = out_ref.shape[0]
    out_iota = lax.broadcasted_iota(jnp.int32, (out_rows, width), 0)
    placed = jnp.zeros((out_rows, width), f32)
    for p in range(n_p):
        mine = (sub < slots) & (lane == p * slots + sub)
        factor = jnp.sum(jnp.where(mine, weight, 0.0), axis=1, keepdims=True)
        block = row_all[p][:, :width]
        scaled = (block * factor).astype(bf16).astype(f32)
        for s in range(slots):
            flag = block[slots + s:slots + s + 1] > 0.5
            hit = (out_iota == offset_ref[0, p] + s) & flag
            placed = jnp.where(hit, scaled[s:s + 1], placed)
    out_ref[...] = placed.astype(bf16)


def fused(n_p, n_f, slab, centres, labels, sample_rows, sample_count, slot_offset):
    rows_pts, width = slab.shape
    rows_dev = rows_pts // n_f
    centre_count, depth = centres.shape
    slots = sample_rows.shape[2]
    chunks = rows_dev // CHUNK
    tiles = centre_count // TILE
    n = n_p * n_f
    wide = pl.cdiv(width, LANES) * LANES
    rows_in = sample_rows.transpose(0, 2, 1)
    labels_in = labels.reshape(1, -1)
    dma = pltpu.SemaphoreType.DMA
    return pl.pallas_call(
        functools.partial(kernel, n_p, n_f, chunks, TILE),
        out_shape=jax.ShapeDtypeStruct((n_p * slots, width), jnp.bfloat16),
        in_specs=[pl.BlockSpec(memory_space=pl.ANY)] * 6,
        out_specs=pl.BlockSpec(memory_space=pltpu.VMEM),
        scratch_shapes=[
            pltpu.VMEM((centre_count, depth), jnp.bfloat16),
            pltpu.VMEM((centre_count, LANES), jnp.float32),
            pltpu.VMEM((centre_count, CHUNK), jnp.float32),
            pltpu.VMEM((width, rows_pts), jnp.bfloat16),
            pltpu.VMEM((depth, rows_dev), jnp.bfloat16),
            pltpu.VMEM(labels_in.shape, jnp.int32),
            pltpu.SMEM(rows_in.shape, jnp.int32),
            pltpu.SMEM(sample_count.shape, jnp.int32),
            pltpu.SMEM(slot_offset.shape, jnp.int32),
            pltpu.VMEM((1, LANES), jnp.float32),
            pltpu.VMEM((n, 1, LANES), jnp.float32),
            pltpu.VMEM((n_p, SUB, wide), jnp.float32),
            pltpu.VMEM((n_p, SUB, wide), jnp.float32),
            pltpu.VMEM((n_p, 1, LANES), jnp.float32),
            pltpu.VMEM((n, 1, LANES), jnp.float32),
            dma((6,)), dma((tiles,)),
            dma((chunks, n_f - 1)), dma((chunks, n_f - 1)),
            dma((n - 1,)), dma((n - 1,)),
            dma((n_p - 1,)), dma((n_p - 1,)),
            dma((n - 1,)), dma((n - 1,)),
        ],
        compiler_params=pltpu.CompilerParams(collective_id=0, has_side_effects=True),
    )(slab.T, labels_in, rows_in, sample_count, slot_offset, centres)


def solution(mesh):
    n_p, n_f = mesh.shape["pts"], mesh.shape["feat"]

    def body(slab, centres, labels, sample_rows, sample_count, slot_offset):
        rows_dev = slab.shape[0] // n_f
        slots = sample_rows.shape[2]
        fits = (
            slab.shape[1] % 16 == 0 and rows_dev % CHUNK == 0 and centres.shape[0] % TILE == 0
            and n_f == 4 and 2 * slab.shape[1] % LANES == 0 and slab.shape[1] > LANES and rows_dev // CHUNK > 1
            and 3 * n_p * slots <= LANES and n_p * SUB <= LANES and 2 * slots <= SUB
        )
        args = (slab, centres, labels, sample_rows, sample_count, slot_offset)
        return fused(n_p, n_f, *args) if fits else local(*args)

    placed = (
        P("pts", "feat"),
        P(),
        P(("pts", "feat"), None),
        P("pts", None, None),
        P("pts", None),
        P("pts", None),
    )
    return jax.shard_map(
        body, mesh=mesh, in_specs=placed, out_specs=P("pts", "feat"), check_vma=False
    )
```
